32 devices in a mesh: parts: 32 (over z, y, x, core).
Axes of the slice: x: 2, y: 2, z: 4, core: 2. Of those that a mesh axis runs over, the one named last changes fastest.
Arguments:
- features: bfloat16 [65536, 256], P('parts'), may hold values from -32 to 32, as said below
- tile_values: bfloat16 [8192, 128, 128], P('parts'), may hold values from -0.0078125 to 0.009338379
- tile_blocks: int32 [8192, 2], P('parts'), may hold values from 0 to 23, as said below
- tile_count: int32 [32], P('parts'), may hold values from 24 to 256, as said below
- send_rows: int32 [32, 4, 256], P('parts'), may hold values from 0 to 2047, as said below
- recv_index: int32 [32, 1024], P('parts'), may hold values from 0 to 1023, as said below
- layer_weight: bfloat16 [2, 256, 256], replicated, may hold values from -0.375 to 0.375
- norm_gain: float32 [2, 256], replicated, may hold values from 0.1 to 1.9
- norm_shift: float32 [2, 256], replicated, may hold values from -3 to 3
Outputs:
- embedded: bfloat16 [65536, 256], P('parts')
The draws below stay inside these ranges and needn't reach their ends.
Inputs may be any that keep to these rules, and one draw needn't show every extreme that they name: `features`: every entry is finite. `tile_blocks`: column 0 is a row block (0 to 15), column 1 a column block of columns_l. A device's first 16 tiles are the diagonal blocks (t, t) in order; the next 8 tiles have the column blocks 2048 // 128, 17, ... in order; blocks may repeat. `tile_count`: the live tiles are the leading ones of a device's list; some device has all 256 live in every draw. `send_rows`: entry [q, n] lists 256 distinct local rows that device q sends to device q + o[n], o = (1, -1, 2, -2). `recv_index`: each device's row is a permutation.
All inputs are finite; a program needn't handle non-finite values.
Results may differ from the reference program's by a relative error of at most 0.0072.
Values may be sent and summed in bfloat16 or wider, within the bound.
A program may use at most 64 MiB of HBM per device.

```python
import jax
import jax.numpy as jnp
from jax import lax

C = 256
B = 128
LAYERS = 2
NEIGHBOURS = 4
V_DEV = 2048
HALO_DEV = 256
NT_DEV = 256
V_TOT = 65536
TILES = 8192
N_PARTS = 32


def draw_features(key, part):
    key_noise, key_spread, key_mean = jax.random.split(key, 3)
    row_total = V_TOT
    position = jnp.arange(row_total, dtype=jnp.float32) / (row_total - 1)
    fluctuation = jnp.clip(jax.random.normal(key_noise, (row_total, C), jnp.float32), -5.0, 5.0)
    drift = jnp.exp(jnp.log(3.0) * (position - 0.5))
    centre = jax.random.uniform(key_mean, (C,), jnp.float32, -0.3, 0.3)
    spread = jnp.exp(jax.random.uniform(key_spread, (row_total,), jnp.float32, -1.15, 1.15))
    return ((fluctuation + centre[None, :]) * (drift * spread)[:, None]).astype(jnp.bfloat16)


def draw_tile_blocks(key, part):
    key_rows, key_cols = jax.random.split(jax.random.fold_in(key, 11), 2)
    row_count = V_DEV // B
    halo_count = NEIGHBOURS * HALO_DEV // B
    number = jnp.arange(TILES, dtype=jnp.int32) % NT_DEV
    random_rows = jax.random.randint(key_rows, (TILES,), 0, row_count, dtype=jnp.int32)
    random_cols = jax.random.randint(key_cols, (TILES,), 0, row_count + halo_count, dtype=jnp.int32)
    diagonal = number < row_count
    halo_part = (number >= row_count) & (number < row_count + halo_count)
    rows_out = jnp.where(diagonal, number, random_rows)
    cols_out = jnp.where(diagonal, number, jnp.where(halo_part, number, random_cols))
    return jnp.stack([rows_out, cols_out], axis=1).astype(jnp.int32)


def draw_tile_count(key, part):
    key_load, key_heavy = jax.random.split(jax.random.fold_in(key, 23), 2)
    device_total = TILES // NT_DEV
    fixed_part = V_DEV // B + NEIGHBOURS * HALO_DEV // B
    remainder = NT_DEV - fixed_part
    drawn = jax.random.randint(key_load, (device_total,), 0, remainder + 1, dtype=jnp.int32)
    skewed = drawn * drawn // remainder
    heaviest = jax.random.randint(key_heavy, (), 0, device_total, dtype=jnp.int32)
    skewed = jnp.where(jnp.arange(device_total, dtype=jnp.int32) == heaviest, remainder, skewed)
    return (fixed_part + skewed).astype(jnp.int32)


def draw_send_rows(key, part):
    device_total = V_TOT // V_DEV
    key_list = jax.random.split(jax.random.fold_in(key, 37), device_total * NEIGHBOURS)
    chosen = jax.vmap(lambda single: jax.random.permutation(single, V_DEV)[:HALO_DEV])(key_list)
    return chosen.reshape(device_total, NEIGHBOURS, HALO_DEV).astype(jnp.int32)


def draw_recv_index(key, part):
    device_total = V_TOT // V_DEV
    key_list = jax.random.split(jax.random.fold_in(key, 41), device_total)
    chosen = jax.vmap(lambda single: jax.random.permutation(single, NEIGHBOURS * HALO_DEV))(key_list)
    return chosen.astype(jnp.int32)


def shard_levels(stream_key, extent, cuts, smallest, high):
    def one(dim, blocks):
        steps = jax.random.uniform(jax.random.fold_in(jax.random.fold_in(stream_key, 6), dim), (blocks,), jnp.float32, smallest / len(cuts), high / len(cuts))
        return jnp.repeat(jnp.exp(steps), extent[dim] // blocks).reshape((-1,) + (1,) * (len(extent) - dim - 1))

    gain = one(*cuts[0])
    for cut in cuts[1:]:
        gain = gain * one(*cut)
    return gain


def centred(stream_key, dims, scale, reach, kind=jnp.bfloat16):
    result = jax.random.normal(stream_key, dims, jnp.float32) * scale
    return jnp.minimum(jnp.maximum(result, -reach), reach).astype(kind)


def setup_inputs(seed: int = 0) -> dict:
    streams_of = jax.random.split(jax.random.key(seed), 10)
    return {
        "features": draw_features(jax.random.fold_in(streams_of[9], 71), 0),
        "tile_values": jnp.clip(-0.0078125 + 0.017150879 * jax.random.uniform(streams_of[1], (TILES, B, B), jnp.float32) ** shard_levels(streams_of[1], (TILES, B, B), ((0, 32),), -0.2, 0.2), -0.0078125, 0.009338379).astype(jnp.bfloat16),
        "tile_blocks": draw_tile_blocks(jax.random.fold_in(streams_of[9], 71), 0),
        "tile_count": draw_tile_count(jax.random.fold_in(streams_of[9], 71), 0),
        "send_rows": draw_send_rows(jax.random.fold_in(streams_of[9], 71), 0),
        "recv_index": draw_recv_index(jax.random.fold_in(streams_of[9], 71), 0),
        "layer_weight": centred(streams_of[6], (LAYERS, C, C), C ** -0.5, 0.375),
        "norm_gain": jnp.clip(1.0 + 0.18 * jax.random.normal(streams_of[7], (LAYERS, C), jnp.float32), 0.1, 1.9),
        "norm_shift": centred(streams_of[8], (LAYERS, C), 0.5, 3.0, jnp.float32),
    }


neighbour_offsets = (1, -1, 2, -2)
norm_eps = 1e-05

def halo_rows(stacked, send_rows, recv_index, device):
    device_total = stacked.shape[0]
    pieces = []
    for position, offset in enumerate(neighbour_offsets):
        source = device - offset
        inside = (source >= 0) & (source < device_total)
        clipped = jnp.clip(source, 0, device_total - 1).astype(jnp.int32)
        source_rows = stacked[clipped]
        picked = jnp.take(source_rows, send_rows[clipped, position], axis=0)
        pieces.append(jnp.where(inside, picked, jnp.zeros_like(picked)))
    received = jnp.concatenate(pieces, axis=0)
    return jnp.take(received, recv_index[device], axis=0)

def aggregate(columns, values, blocks, live_count):
    tile_edge = values.shape[1]
    channels = columns.shape[1]
    column_blocks = columns.reshape(-1, tile_edge, channels)
    picked = jnp.take(column_blocks, blocks[:, 1], axis=0).astype(jnp.float32)
    partial_value = jnp.einsum('tij,tjc->tic', values.astype(jnp.float32), picked, precision=lax.Precision.HIGHEST)
    row_count = V_DEV // B
    owners = (blocks[:, 0][None, :] == jnp.arange(row_count, dtype=jnp.int32)[:, None]) & (jnp.arange(values.shape[0], dtype=jnp.int32) < live_count)[None, :]
    summed = jnp.einsum('rt,tic->ric', owners.astype(jnp.float32), partial_value, precision=lax.Precision.HIGHEST)
    return summed.reshape(row_count * tile_edge, channels)

def reference(features, tile_values, tile_blocks, tile_count, send_rows, recv_index, layer_weight, norm_gain, norm_shift):
    stacked = features.reshape(N_PARTS, V_DEV, C)
    values_all = tile_values.reshape(N_PARTS, NT_DEV, B, B)
    blocks_all = tile_blocks.reshape(N_PARTS, NT_DEV, 2)
    for layer_index in range(LAYERS):
        weight = layer_weight[layer_index]

        def one_device(device, stacked=stacked, weight=weight):
            halo_block = halo_rows(stacked, send_rows, recv_index, device)
            columns = jnp.concatenate([stacked[device], halo_block], axis=0)
            summed = aggregate(columns, values_all[device], blocks_all[device], tile_count[device])
            gathered = summed.astype(jnp.bfloat16)
            return jnp.dot(gathered, weight, preferred_element_type=jnp.float32).astype(jnp.bfloat16)
        mixed_rows = lax.map(one_device, jnp.arange(N_PARTS, dtype=jnp.int32))
        widened = mixed_rows.astype(jnp.float32)
        centre = lax.optimization_barrier(jnp.mean(widened, axis=(0, 1)))
        spread = lax.optimization_barrier(jnp.mean(jnp.square(widened - centre), axis=(0, 1)))
        scaled = (widened - centre) / jnp.sqrt(spread + norm_eps)
        stacked = jax.nn.relu(norm_gain[layer_index] * scaled + norm_shift[layer_index]).astype(jnp.bfloat16)
    return stacked.reshape(V_TOT, C)
```

```python
import functools

import jax
import jax.numpy as jnp
from jax import lax
from jax.experimental import pallas as pl
from jax.experimental.pallas import tpu as pltpu
from jax.sharding import PartitionSpec as P

neighbour_offsets = (1, -1, 2, -2)
norm_eps = 1e-05
MESH = pl.DeviceIdType.MESH


def plan(tile_blocks, live_count, row_count, group_total):
    tile_total = tile_blocks.shape[0]
    number = jnp.arange(tile_total, dtype=jnp.int32)
    live = number < live_count
    rows = jnp.where(live, tile_blocks[:, 0], row_count)
    same = rows[:, None] == rows[None, :]
    rank = jnp.sum((same & (number[None, :] < number[:, None])).astype(jnp.int32), axis=1)
    blocks = jnp.arange(row_count, dtype=jnp.int32)
    counts = jnp.sum((rows[None, :] == blocks[:, None]).astype(jnp.int32), axis=1)
    groups = (counts + 1) // 2
    start = jnp.sum(jnp.where(blocks[None, :] < blocks[:, None], groups[None, :], 0), axis=1)
    first = jnp.sum(jnp.where(rows[:, None] == blocks[None, :], start[None, :], 0), axis=1)
    slot = jnp.where(live, 2 * first + rank, -1)
    hit = jnp.arange(2 * group_total, dtype=jnp.int32)[:, None] == slot[None, :]
    tile_of = tile_total + jnp.sum(jnp.where(hit, number[None, :] - tile_total, 0), axis=1)
    column_of = jnp.sum(jnp.where(hit, tile_blocks[:, 1][None, :], 0), axis=1)
    group_number = jnp.arange(group_total, dtype=jnp.int32)
    keep = 1.0 - jnp.sum((group_number[:, None] == start[None, :]).astype(jnp.float32), axis=1)
    return tile_of, column_of, keep, start + groups - 1


def kernel(
    n,
    tile_of,
    column_of,
    keep,
    last_of,
    send_rows,
    recv_index,
    weight,
    gain,
    shift,
    features,
    tile_values,
    out,
    tiles,
    columns,
    pick,
    order,
    run,
    mixed,
    outgoing,
    received,
    stats,
    tile_sem,
    feature_sem,
    out_sem,
    halo_send,
    halo_recv,
    stat_send,
    stat_recv,
):
    me = lax.axis_index("parts")
    layers = weight.shape[0]
    tile_total, edge, _ = tile_values.shape
    row_count, _, channels = out.shape
    vertices = row_count * edge
    halo_count = received.shape[2]
    group_total = keep.shape[0]
    neighbours = len(neighbour_offsets)

    feature_copy = pltpu.make_async_copy(features, columns.at[pl.ds(0, row_count)], feature_sem)
    feature_copy.start()
    tile_copy = pltpu.make_async_copy(tile_values, tiles.at[pl.ds(0, tile_total)], tile_sem)
    tile_copy.start()

    barrier = pltpu.get_barrier_semaphore()

    def greet(step, carry):
        pl.semaphore_signal(
            barrier, inc=1, device_id=(lax.rem(me + step, n),), device_id_type=MESH
        )
        return carry

    lax.fori_loop(1, n, greet, 0)

    tiles[tile_total] = jnp.zeros((edge, tiles.shape[2]), tiles.dtype)
    for position, offset in enumerate(neighbour_offsets):
        source = me - offset

        @pl.when((source < 0) | (source >= n))
        def _():
            for layer in range(layers):
                received[layer, position] = jnp.zeros((halo_count, channels), received.dtype)

    lane = lax.broadcasted_iota(jnp.int32, (128, 128), 1)

    def one_hot(index_row, target, first_row, width):
        spread = jnp.broadcast_to(index_row, (128, 128)).T
        for chunk in range(width // 128):
            found = spread == lane + chunk * 128
            target[pl.ds(first_row, 128), pl.ds(chunk * 128, 128)] = jnp.where(
                found, 1.0, 0.0
            ).astype(jnp.bfloat16)

    for position in range(neighbours):
        for half in range(halo_count // 128):
            one_hot(
                send_rows[0, pl.ds(position, 1), pl.ds(half * 128, 128)],
                pick,
                position * halo_count + half * 128,
                vertices,
            )
    feature_copy.wait()

    def halo_copy(layer, position, device):
        return pltpu.make_async_remote_copy(
            src_ref=outgoing.at[layer, position],
            dst_ref=received.at[layer, position],
            send_sem=halo_send.at[layer, position],
            recv_sem=halo_recv.at[layer, position],
            device_id=(device,),
            device_id_type=MESH,
        )

    def stat_copy(layer, step, device):
        return pltpu.make_async_remote_copy(
            src_ref=stats.at[layer, me],
            dst_ref=stats.at[layer, me],
            send_sem=stat_send.at[layer, step],
            recv_sem=stat_recv.at[layer, step],
            device_id=(device,),
            device_id_type=MESH,
        )

    for layer in range(layers):
        for position, offset in enumerate(neighbour_offsets):
            outgoing[layer, position] = jnp.dot(
                pick[pl.ds(position * halo_count, halo_count), :],
                columns[pl.ds(0, row_count)].reshape(vertices, channels),
                preferred_element_type=jnp.float32,
            ).astype(jnp.bfloat16)
        if layer == 0:
            pl.semaphore_wait(barrier, n - 1)
        for position, offset in enumerate(neighbour_offsets):
            target = me + offset

            @pl.when((target >= 0) & (target < n))
            def _():
                halo_copy(layer, position, target).start()

        if layer == 0:
            for part in range(neighbours * halo_count // 128):
                one_hot(
                    recv_index[pl.ds(0, 1), pl.ds(part * 128, 128)],
                    order,
                    part * 128,
                    neighbours * halo_count,
                )
        for position, offset in enumerate(neighbour_offsets):
            source = me - offset

            @pl.when((source >= 0) & (source < n))
            def _():
                halo_copy(layer, position, me).wait_recv()

        arrived = received[layer].reshape(neighbours * halo_count, channels)
        columns[pl.ds(row_count, neighbours * halo_count // edge)] = (
            jnp.dot(order[...], arrived, preferred_element_type=jnp.float32)
            .astype(jnp.bfloat16)
            .reshape(neighbours * halo_count // edge, edge, channels)
        )
        if layer == 0:
            tile_copy.wait()

        unroll = 4 if group_total % 4 == 0 else 1

        def sweep(turn, total):
            for step in range(unroll):
                group = turn * unroll + step
                values = jnp.concatenate(
                    [tiles[tile_of[2 * group]], tiles[tile_of[2 * group + 1]]], axis=1
                )
                picked = [columns[column_of[2 * group + k]] for k in range(2)]
                total = total * keep[group] + jnp.dot(
                    values, jnp.concatenate(picked, axis=0), preferred_element_type=jnp.float32
                )
                run[group] = total.astype(jnp.bfloat16)
            return total

        lax.fori_loop(
            0, group_total // unroll, sweep, jnp.zeros((edge, channels), jnp.float32)
        )

        def mix(block, carry):
            sums, squares = carry
            product = jnp.dot(
                run[last_of[block]], weight[layer], preferred_element_type=jnp.float32
            ).astype(jnp.bfloat16)
            mixed[block] = product
            wide = product.astype(jnp.float32).reshape(edge // 8, 8, channels)
            return sums + jnp.sum(wide, axis=0), squares + jnp.sum(wide * wide, axis=0)

        nothing = jnp.zeros((8, channels), jnp.float32)
        sums, squares = lax.fori_loop(0, row_count, mix, (nothing, nothing))
        stats[layer, me] = jnp.concatenate(
            [jnp.sum(sums, axis=0, keepdims=True), jnp.sum(squares, axis=0, keepdims=True)], axis=0
        )

        def share(step, carry):
            stat_copy(layer, step, lax.rem(me + step, n)).start()
            return carry

        lax.fori_loop(1, n, share, 0)

        for position, offset in enumerate(neighbour_offsets):
            target = me + offset

            @pl.when((target >= 0) & (target < n))
            def _():
                halo_copy(layer, position, target).wait_send()

        def collect(step, carry):
            pltpu.make_async_remote_copy(
                src_ref=stats.at[layer, me],
                dst_ref=stats.at[layer, lax.rem(me + n - step, n)],
                send_sem=stat_send.at[layer, step],
                recv_sem=stat_recv.at[layer, step],
                device_id=(lax.rem(me + step, n),),
                device_id_type=MESH,
            ).wait()
            return carry

        lax.fori_loop(1, n, collect, 0)
        both = jnp.sum(stats[layer], axis=0) / (vertices * n)
        centre = both[0:1]
        spread = jnp.maximum(both[1:2] - centre * centre, 0.0)
        scale = gain[pl.ds(layer, 1), :] / jnp.sqrt(spread + norm_eps)
        base = shift[pl.ds(layer, 1), :]

        def normalise(block, carry):
            wide = mixed[block].astype(jnp.float32)
            columns[block] = jnp.maximum((wide - centre) * scale + base, 0.0).astype(
                jnp.bfloat16
            )
            return carry

        lax.fori_loop(0, row_count, normalise, 0)

    out_copy = pltpu.make_async_copy(columns.at[pl.ds(0, row_count)], out, out_sem)
    out_copy.start()
    out_copy.wait()


def shards(
    n,
    features,
    tile_values,
    tile_blocks,
    tile_count,
    send_rows,
    recv_index,
    layer_weight,
    norm_gain,
    norm_shift,
):
    tile_total, edge, depth = tile_values.shape
    vertices, channels = features.shape
    row_count = vertices // edge
    layers = layer_weight.shape[0]
    neighbours, halo_count = send_rows.shape[1:]
    group_total = (tile_total + row_count + 1) // 2
    group_total = (group_total + 3) // 4 * 4
    tables = plan(tile_blocks, tile_count[0], row_count, group_total)
    smem = pl.BlockSpec(memory_space=pltpu.SMEM)
    vmem = pl.BlockSpec(memory_space=pltpu.VMEM)
    anywhere = pl.BlockSpec(memory_space=pl.ANY)
    bf16, f32 = jnp.bfloat16, jnp.float32
    result = pl.pallas_call(
        functools.partial(kernel, n),
        out_shape=jax.ShapeDtypeStruct((row_count, edge, channels), bf16),
        in_specs=[smem] * 4 + [vmem] * 5 + [anywhere] * 2,
        out_specs=anywhere,
        scratch_shapes=[
            pltpu.VMEM((tile_total + 1, edge, depth), bf16),
            pltpu.VMEM((row_count + neighbours * halo_count // edge, edge, channels), bf16),
            pltpu.VMEM((neighbours * halo_count, vertices), bf16),
            pltpu.VMEM((neighbours * halo_count, neighbours * halo_count), bf16),
            pltpu.VMEM((group_total, edge, channels), bf16),
            pltpu.VMEM((row_count, edge, channels), bf16),
            pltpu.VMEM((layers, neighbours, halo_count, channels), bf16),
            pltpu.VMEM((layers, neighbours, halo_count, channels), bf16),
            pltpu.VMEM((layers, n, 2, channels), f32),
            pltpu.SemaphoreType.DMA,
            pltpu.SemaphoreType.DMA,
            pltpu.SemaphoreType.DMA,
            pltpu.SemaphoreType.DMA((layers, neighbours)),
            pltpu.SemaphoreType.DMA((layers, neighbours)),
            pltpu.SemaphoreType.DMA((layers, n)),
            pltpu.SemaphoreType.DMA((layers, n)),
        ],
        compiler_params=pltpu.CompilerParams(
            collective_id=0, has_side_effects=True, vmem_limit_bytes=56 * 2**20
        ),
    )(
        *tables,
        send_rows,
        recv_index,
        layer_weight,
        norm_gain,
        norm_shift,
        features.reshape(row_count, edge, channels),
        tile_values,
    )
    return result.reshape(vertices, channels)


def solution(mesh):
    return jax.shard_map(
        functools.partial(shards, mesh.shape["parts"]),
        mesh=mesh,
        in_specs=(
            P("parts", None),
            P("parts", None, None),
            P("parts", None),
            P("parts"),
            P("parts", None, None),
            P("parts", None),
            P(),
            P(),
            P(),
        ),
        out_specs=P("parts", None),
        check_vma=False,
    )
```

```python
import functools

import jax
import jax.numpy as jnp
from jax import lax
from jax.experimental import pallas as pl
from jax.experimental.pallas import tpu as pltpu
from jax.sharding import PartitionSpec as P

neighbour_offsets = (1, -1, 2, -2)
norm_eps = 1e-05
MESH = pl.DeviceIdType.MESH


def kernel(
    n,
    tile_count,
    tile_blocks,
    send_rows,
    recv_index,
    weight,
    gain,
    shift,
    features,
    tile_values,
    out,
    affine,
    tiles,
    columns,
    pick,
    order,
    run,
    dense,
    partial,
    mixed,
    outgoing,
    received,
    stats,
    table,
    table_smem,
    tile_sem,
    feature_sem,
    table_sem,
    out_sem,
    halo_send,
    halo_recv,
    stat_send,
    stat_recv,
):
    me = lax.axis_index("parts")
    layers = weight.shape[0]
    tile_total, edge, _ = tile_values.shape
    row_count, _, channels = out.shape
    vertices = row_count * edge
    halo_count = received.shape[2]
    neighbours = len(neighbour_offsets)
    halo_rows = neighbours * halo_count
    column_count = (vertices + halo_rows) // edge
    cell_total = row_count * column_count

    feature_copy = pltpu.make_async_copy(features, columns.at[pl.ds(0, row_count)], feature_sem)
    feature_copy.start()
    tile_copy = pltpu.make_async_copy(tile_values, tiles, tile_sem)
    tile_copy.start()

    barrier = pltpu.get_barrier_semaphore()

    def greet(step, carry):
        pl.semaphore_signal(
            barrier, inc=1, device_id=(lax.rem(me + step, n),), device_id_type=MESH
        )
        return carry

    lax.fori_loop(1, n, greet, 0)

    for position, offset in enumerate(neighbour_offsets):
        source = me - offset

        @pl.when((source < 0) | (source >= n))
        def _():
            for layer in range(layers):
                received[layer, position] = jnp.zeros((halo_count, channels), received.dtype)

    lane = lax.broadcasted_iota(jnp.int32, (128, 128), 1)

    def upright(row):
        return jnp.broadcast_to(row, (128, 128)).T

    def one_hot(index_row, target, first_row, width):
        spread = upright(index_row)
        for chunk in range(width // 128):
            found = spread == lane + chunk * 128
            target[pl.ds(first_row, 128), pl.ds(chunk * 128, 128)] = jnp.where(
                found, 1.0, 0.0
            ).astype(jnp.bfloat16)

    for position in range(neighbours):
        for half in range(halo_count // 128):
            one_hot(
                send_rows[0, pl.ds(position, 1), pl.ds(half * 128, 128)],
                pick,
                position * halo_count + half * 128,
                vertices,
            )
    feature_copy.wait()

    def halo_copy(layer, position, device):
        return pltpu.make_async_remote_copy(
            src_ref=outgoing.at[layer, position],
            dst_ref=received.at[layer, position],
            send_sem=halo_send.at[layer, position],
            recv_sem=halo_recv.at[layer, position],
            device_id=(device,),
            device_id_type=MESH,
        )

    def gather_rows(layer, position):
        outgoing[layer, position] = jnp.dot(
            pick[pl.ds(position * halo_count, halo_count), :],
            columns[pl.ds(0, row_count)].reshape(vertices, channels),
            preferred_element_type=jnp.float32,
        ).astype(jnp.bfloat16)

    def send_halo(layer, position):
        target = me + neighbour_offsets[position]

        @pl.when((target >= 0) & (target < n))
        def _():
            halo_copy(layer, position, target).start()

    count = tile_count[0]
    spans = tile_total // 128
    low = lax.broadcasted_iota(jnp.int32, (1, 128), 1)
    cells, keys = [], []
    for span in range(spans):
        place = pl.ds(span * 128, 128)
        number = low + span * 128
        cell = tile_blocks[pl.ds(0, 1), place] * column_count + tile_blocks[pl.ds(1, 1), place]
        cell = jnp.where(number < count, cell, cell_total)
        cells.append(cell)
        keys.append(cell * tile_total + number)
    tall_cells = [upright(cell) for cell in cells]
    tall_keys = [upright(key) for key in keys]

    def total_over(terms):
        return jnp.sum(functools.reduce(jnp.add, terms), axis=0, keepdims=True)

    def flag(condition):
        return jnp.where(condition, 1, 0)

    slots, repeats = [], []
    for span in range(spans):
        slots.append(total_over([flag(tall < keys[span]) for tall in tall_keys]))
        repeats.append(
            total_over(
                [
                    flag((tall < keys[span]) & (tall_cell == cells[span]))
                    for tall, tall_cell in zip(tall_keys, tall_cells)
                ]
            )
        )
    tall_slots = [upright(slot) for slot in slots]
    tall_repeats = [upright(jnp.minimum(repeat, 1)) for repeat in repeats]
    upward = lax.broadcasted_iota(jnp.int32, (128, 128), 0)
    for span in range(spans):
        here = [tall == low + span * 128 for tall in tall_slots]
        table[pl.ds(0, 1), pl.ds(span * 128, 128)] = total_over(
            [jnp.where(hit, upward + k * 128, 0) for k, hit in enumerate(here)]
        )
        table[pl.ds(0, 1), pl.ds(tile_total + span * 128, 128)] = total_over(
            [jnp.where(hit, tall, 0) for hit, tall in zip(here, tall_repeats)]
        )
    for span in range(cell_total // 128):
        cell = low + span * 128
        reached = total_over([flag(tall <= cell) for tall in tall_cells])
        present = total_over([flag(tall == cell) for tall in tall_cells])
        table[pl.ds(0, 1), pl.ds(2 * tile_total + span * 128, 128)] = jnp.where(
            present > 0, reached - 1, tile_total
        )

    for position in range(neighbours):
        gather_rows(0, position)
    table_copy = pltpu.make_async_copy(table, table_smem, table_sem)
    table_copy.start()
    pl.semaphore_wait(barrier, n - 1)
    for position in range(neighbours):
        send_halo(0, position)
    for part in range(halo_rows // 128):
        one_hot(recv_index[pl.ds(0, 1), pl.ds(part * 128, 128)], order, part * 128, halo_rows)
    table_copy.wait()
    tile_copy.wait()

    run[tile_total] = jnp.zeros((edge, edge), run.dtype)
    unroll = 4

    def sweep(turn, total):
        for step in range(unroll):
            slot = turn * unroll + step
            kept = table_smem[0, tile_total + slot].astype(jnp.float32)
            total = total * kept + tiles[table_smem[0, slot]].astype(jnp.float32)
            run[slot] = total.astype(jnp.bfloat16)
        return total

    lax.fori_loop(0, tile_total // unroll, sweep, jnp.zeros((edge, edge), jnp.float32))

    def lay(block, carry):
        place = pl.ds(pl.multiple_of(block * edge, edge), edge)
        for column in range(column_count):
            dense[place, pl.ds(column * edge, edge)] = run[
                table_smem[0, 2 * tile_total + block * column_count + column]
            ]
        return carry

    lax.fori_loop(0, row_count, lay, 0)

    chunk_rows = 4 * edge if row_count % 4 == 0 else edge
    chunks = vertices // chunk_rows

    for layer in range(layers):
        if layer > 0:
            for position in range(neighbours):
                gather_rows(layer, position)
                send_halo(layer, position)
        for chunk in range(chunks):
            place = pl.ds(chunk * chunk_rows, chunk_rows)
            partial[place, :] = jnp.dot(
                dense[place, pl.ds(0, vertices)],
                columns[pl.ds(0, row_count)].reshape(vertices, channels),
                preferred_element_type=jnp.float32,
            )
        for position, offset in enumerate(neighbour_offsets):
            source = me - offset

            @pl.when((source >= 0) & (source < n))
            def _():
                halo_copy(layer, position, me).wait_recv()

        halo = jnp.dot(
            order[...],
            received[layer].reshape(halo_rows, channels),
            preferred_element_type=jnp.float32,
        ).astype(jnp.bfloat16)
        columns[pl.ds(row_count, halo_rows // edge)] = halo.reshape(
            halo_rows // edge, edge, channels
        )
        sums = jnp.zeros((8, channels), jnp.float32)
        squares = jnp.zeros((8, channels), jnp.float32)
        for chunk in range(chunks):
            place = pl.ds(chunk * chunk_rows, chunk_rows)
            summed = partial[place, :] + jnp.dot(
                dense[place, pl.ds(vertices, halo_rows)],
                columns[pl.ds(row_count, halo_rows // edge)].reshape(halo_rows, channels),
                preferred_element_type=jnp.float32,
            )
            product = jnp.dot(
                summed.astype(jnp.bfloat16), weight[layer], preferred_element_type=jnp.float32
            ).astype(jnp.bfloat16)
            mixed[pl.ds(chunk * chunk_rows // edge, chunk_rows // edge)] = product.reshape(
                chunk_rows // edge, edge, channels
            )
            wide = product.astype(jnp.float32).reshape(chunk_rows // 8, 8, channels)
            sums = sums + jnp.sum(wide, axis=0)
            squares = squares + jnp.sum(wide * wide, axis=0)
        stats[layer, me] = jnp.concatenate(
            [jnp.sum(sums, axis=0, keepdims=True), jnp.sum(squares, axis=0, keepdims=True)], axis=0
        )

        def share(step, carry):
            pltpu.make_async_remote_copy(
                src_ref=stats.at[layer, me],
                dst_ref=stats.at[layer, me],
                send_sem=stat_send.at[layer, step],
                recv_sem=stat_recv.at[layer, step],
                device_id=(lax.rem(me + step, n),),
                device_id_type=MESH,
            ).start()
            return carry

        lax.fori_loop(1, n, share, 0)
        last = layer == layers - 1
        if last:
            out_copy = pltpu.make_async_copy(mixed, out, out_sem)
            out_copy.start()

        for position, offset in enumerate(neighbour_offsets):
            target = me + offset

            @pl.when((target >= 0) & (target < n))
            def _():
                halo_copy(layer, position, target).wait_send()

        def collect(step, carry):
            pltpu.make_async_remote_copy(
                src_ref=stats.at[layer, me],
                dst_ref=stats.at[layer, lax.rem(me + n - step, n)],
                send_sem=stat_send.at[layer, step],
                recv_sem=stat_recv.at[layer, step],
                device_id=(lax.rem(me + step, n),),
                device_id_type=MESH,
            ).wait()
            return carry

        lax.fori_loop(1, n, collect, 0)
        both = jnp.sum(stats[layer], axis=0) / (vertices * n)
        centre = both[0:1]
        spread = jnp.maximum(both[1:2] - centre * centre, 0.0)
        scale = gain[pl.ds(layer, 1), :] / jnp.sqrt(spread + norm_eps)
        base = shift[pl.ds(layer, 1), :]
        if last:
            affine[...] = jnp.concatenate([centre, scale], axis=0)
            out_copy.wait()
        else:
            for block in range(row_count):
                wide = mixed[block].astype(jnp.float32)
                columns[block] = jnp.maximum((wide - centre) * scale + base, 0.0).astype(
                    jnp.bfloat16
                )


def shards(
    n,
    features,
    tile_values,
    tile_blocks,
    tile_count,
    send_rows,
    recv_index,
    layer_weight,
    norm_gain,
    norm_shift,
):
    tile_total, edge, depth = tile_values.shape
    vertices, channels = features.shape
    row_count = vertices // edge
    layers = layer_weight.shape[0]
    neighbours, halo_count = send_rows.shape[1:]
    halo_rows = neighbours * halo_count
    table_size = 2 * tile_total + row_count * (row_count + halo_rows // edge)
    smem = pl.BlockSpec(memory_space=pltpu.SMEM)
    vmem = pl.BlockSpec(memory_space=pltpu.VMEM)
    anywhere = pl.BlockSpec(memory_space=pl.ANY)
    bf16, f32 = jnp.bfloat16, jnp.float32
    mixed, affine = pl.pallas_call(
        functools.partial(kernel, n),
        out_shape=(
            jax.ShapeDtypeStruct((row_count, edge, channels), bf16),
            jax.ShapeDtypeStruct((2, channels), f32),
        ),
        in_specs=[smem] + [vmem] * 6 + [anywhere] * 2,
        out_specs=(anywhere, vmem),
        scratch_shapes=[
            pltpu.VMEM((tile_total, edge, depth), bf16),
            pltpu.VMEM((row_count + halo_rows // edge, edge, channels), bf16),
            pltpu.VMEM((halo_rows, vertices), bf16),
            pltpu.VMEM((halo_rows, halo_rows), bf16),
            pltpu.VMEM((tile_total + 1, edge, depth), bf16),
            pltpu.VMEM((vertices, vertices + halo_rows), bf16),
            pltpu.VMEM((vertices, channels), f32),
            pltpu.VMEM((row_count, edge, channels), bf16),
            pltpu.VMEM((layers, neighbours, halo_count, channels), bf16),
            pltpu.VMEM((layers, neighbours, halo_count, channels), bf16),
            pltpu.VMEM((layers, n, 2, channels), f32),
            pltpu.VMEM((1, table_size), jnp.int32),
            pltpu.SMEM((1, table_size), jnp.int32),
            pltpu.SemaphoreType.DMA,
            pltpu.SemaphoreType.DMA,
            pltpu.SemaphoreType.DMA,
            pltpu.SemaphoreType.DMA,
            pltpu.SemaphoreType.DMA((layers, neighbours)),
            pltpu.SemaphoreType.DMA((layers, neighbours)),
            pltpu.SemaphoreType.DMA((layers, n)),
            pltpu.SemaphoreType.DMA((layers, n)),
        ],
        compiler_params=pltpu.CompilerParams(
            collective_id=0, has_side_effects=True, vmem_limit_bytes=56 * 2**20
        ),
    )(
        tile_count,
        tile_blocks.T,
        send_rows,
        recv_index,
        layer_weight,
        norm_gain,
        norm_shift,
        features.reshape(row_count, edge, channels),
        tile_values,
    )
    wide = mixed.reshape(vertices, channels).astype(f32)
    return jax.nn.relu((wide - affine[0]) * affine[1] + norm_shift[layers - 1]).astype(bf16)


def solution(mesh):
    return jax.shard_map(
        functools.partial(shards, mesh.shape["parts"]),
        mesh=mesh,
        in_specs=(
            P("parts", None),
            P("parts", None, None),
            P("parts", None),
            P("parts"),
            P("parts", None, None),
            P("parts", None),
            P(),
            P(),
            P(),
        ),
        out_specs=P("parts", None),
        check_vma=False,
    )
```
